32 devices in a mesh: rep: 8 (over z, core), mdl: 4 (over y, x).
Axes of the slice: x: 2, y: 2, z: 4, core: 2. Of those that a mesh axis runs over, the one named last changes fastest.
Arguments:
- deltas: bfloat16 [8, 2560, 2560], P('rep', 'mdl'), may hold values from -72 to 72
- errors: bfloat16 [8, 2560, 2560], P('rep', 'mdl'), may hold values from -3 to 3
- starts: float32 [2560, 64], replicated, may hold values from -6 to 6
- momentum: float32 [2560, 2560], P('mdl', 'rep'), may hold values from -2 to 2
Outputs:
- new_errors: bfloat16 [8, 2560, 2560], P('rep', 'mdl')
- new_momentum: float32 [2560, 2560], P('mdl', 'rep')
- outer_step: float32 [2560, 2560], P('mdl', 'rep')
The draws below stay inside these ranges and needn't reach their ends.
All inputs are finite; a program needn't handle non-finite values.
Results may differ from the reference program's by a relative error of at most 0.001.
Values sent between devices are 32-bit elements; how exact they have to be, the bound alone decides.
A program may use at most 64 MiB of HBM per device.

```python
import math
import jax
import jax.numpy as jnp
from jax import lax

CHANNELS = 2560
RANK = 64
REPLICAS = 8


def draw_deltas(key, part):
    keys = jax.random.split(jax.random.fold_in(key, 7), 5)
    shape_one = (CHANNELS, CHANNELS)
    common = jax.random.truncated_normal(keys[0], -4.0, 4.0, shape_one, jnp.float32)
    own = jax.random.truncated_normal(keys[1], -4.0, 4.0, (REPLICAS,) + shape_one, jnp.float32)
    ramp = 1.0 + 2.0 * jnp.arange(REPLICAS, dtype=jnp.float32) / max(REPLICAS - 1, 1)
    replica_scale = ramp * jax.random.uniform(keys[2], (REPLICAS,), jnp.float32, 0.8, 1.2)
    row_ramp = jnp.exp(math.log(3.0) * jnp.arange(CHANNELS, dtype=jnp.float32) / CHANNELS)
    row_scale = jnp.exp(jax.random.uniform(keys[3], (CHANNELS, 1), jnp.float32, math.log(0.3), 0.0)) * row_ramp[:, None]
    column_scale = jnp.exp(jax.random.uniform(keys[4], (1, CHANNELS), jnp.float32, math.log(0.3), math.log(3.0)))
    mixed = 0.3 * common[None] + replica_scale[:, None, None] * own
    return (0.5 * mixed * row_scale[None] * column_scale[None]).astype(jnp.bfloat16)


def block_scale(key, extent, shards, least, high):
    gain, own = 1.0, jax.random.fold_in(key, 6)
    for dim, parts in shards:
        heights = jnp.exp(jax.random.uniform(jax.random.fold_in(own, dim), (parts,), jnp.float32, least / len(shards), high / len(shards)))
        gain = gain * jnp.repeat(heights, extent[dim] // parts).reshape([-1 if axis == dim else 1 for axis in range(len(extent))])
    return gain


def scatter_about(own_key, extent, spread, most, cuts=(), kind=jnp.bfloat16):
    values = jax.random.normal(own_key, extent, jnp.float32) * spread
    if len(cuts) > 0:
        values = block_scale(own_key, extent, cuts, -0.22, 0.18) * values
    return jnp.clip(values, min=-most, max=most).astype(kind)


def setup_inputs(seed: int = 0) -> dict:
    arg_keys = jax.random.split(jax.random.key(seed), 5)
    deltas = draw_deltas(jax.random.fold_in(arg_keys[4], 71), 0)
    errors = scatter_about(arg_keys[1], (REPLICAS, CHANNELS, CHANNELS), 0.5, 3.0, ((0, 8), (1, 4)))
    starts = scatter_about(arg_keys[2], (CHANNELS, RANK), 1.0, 6.0, (), jnp.float32)
    momentum = scatter_about(arg_keys[3], (CHANNELS, CHANNELS), 0.3, 2.0, ((0, 4), (1, 8)), jnp.float32)
    return {"deltas": deltas, "errors": errors, "starts": starts, "momentum": momentum}


def reference(deltas, errors, starts, momentum):
    highest = lax.Precision.HIGHEST

    def left_add(total, pair):
        merged = pair[0].astype(jnp.float32) + pair[1].astype(jnp.float32)
        return (total + jnp.einsum('ac,ck->ka', merged, starts, precision=highest), None)
    left, unused = lax.scan(left_add, jnp.zeros((RANK, CHANNELS), jnp.float32), (deltas, errors))
    left = left / REPLICAS
    gram = jnp.einsum('ka,la->kl', left, left, precision=highest)
    lower = jnp.linalg.cholesky(gram)
    basis = jax.scipy.linalg.solve_triangular(lower, left, lower=True)

    def right_add(total, pair):
        merged = pair[0].astype(jnp.float32) + pair[1].astype(jnp.float32)
        return (total + jnp.einsum('ac,ka->kc', merged, basis, precision=highest), None)
    right, unused = lax.scan(right_add, jnp.zeros((RANK, CHANNELS), jnp.float32), (deltas, errors))
    right = right / REPLICAS
    approx = jnp.einsum('ka,kc->ac', basis, right, precision=highest)

    def residue(pair):
        merged = pair[0].astype(jnp.float32) + pair[1].astype(jnp.float32)
        return (merged - approx).astype(jnp.bfloat16)
    new_errors = lax.map(residue, (deltas, errors))
    new_momentum = 0.9 * momentum + approx
    outer_step = 0.7 * (approx + 0.9 * new_momentum)
    return (new_errors, new_momentum, outer_step)
```

```python
import functools

import jax
import jax.numpy as jnp
from jax import lax
from jax.experimental import pallas as pl
from jax.experimental.pallas import tpu as pltpu
from jax.sharding import PartitionSpec as P

MESH = pl.DeviceIdType.MESH
highest = lax.Precision.HIGHEST
f32, bf16 = jnp.float32, jnp.bfloat16


def split3(x):
    hi = x.astype(bf16)
    rest = x - hi.astype(f32)
    mid = rest.astype(bf16)
    return hi, mid, (rest - mid.astype(f32)).astype(bf16)


def split2(x):
    hi = x.astype(bf16)
    return hi, (x - hi.astype(f32)).astype(bf16)


def when(cond, always):
    if always:
        return lambda f: f()
    return pl.when(cond)


def inverse(g, rank):
    rows = lax.broadcasted_iota(jnp.int32, (rank, rank), 0)
    cols = lax.broadcasted_iota(jnp.int32, (rank, rank), 1)
    for k in range(rank):
        row = g[k : k + 1, :]
        col = g[:, k : k + 1]
        scale = 1.0 / g[k : k + 1, k : k + 1]
        rowk, colk = rows == k, cols == k
        scaled = row * scale
        left = jnp.where(rowk[:, :1], 0.0, col)
        kept = jnp.where(colk, 0.0, g)
        fill = jnp.where(colk[:1, :], scale, scaled)
        g = jnp.where(rowk, fill, kept - left * fill)
    return g


def factors(
    nr, nm, shares, chunk, width,
    d_hbm, e_hbm, s_ref,
    y_ref, r_ref, own_ref,
    dv, ev, lpart, lrecv, lfull, gbuf, rpart, rrecv, rsum, zrecv, rfull,
    in_sem, ls_s, ls_r, lg_s, lg_r, g_s, g_r, rs_s, rs_r, zs_s, zs_r, zg_s, zg_r, rg_s, rg_r,
):
    rep, mdl = lax.axis_index("rep"), lax.axis_index("mdl")
    rank = s_ref.shape[1]
    per = rank // shares
    rows, channels = dv.shape
    cw = channels // nm
    chunks = rows // chunk
    everyone = shares == nr

    def rep_at(d):
        return lax.rem(rep + d + nr, nr)

    def mdl_at(d):
        return lax.rem(mdl + d + nm, nm)

    loads = []
    for i in range(chunks):
        span = pl.ds(i * chunk, chunk)
        pair = (
            pltpu.make_async_copy(d_hbm.at[span], dv.at[span], in_sem.at[0, i]),
            pltpu.make_async_copy(e_hbm.at[span], ev.at[span], in_sem.at[1, i]),
        )
        for c in pair:
            c.start()
        loads.append(pair)

    barrier = pltpu.get_barrier_semaphore()
    for d in range(1, nr):
        pl.semaphore_signal(barrier, inc=1, device_id=(rep_at(d), mdl), device_id_type=MESH)
    for d in range(1, nm):
        pl.semaphore_signal(barrier, inc=1, device_id=(rep, mdl_at(d)), device_id_type=MESH)

    s3 = jnp.concatenate(split3(s_ref[...].T), axis=0)
    nt = (((1,), (1,)), ((), ()))

    def fold(x):
        return x[:rank] + (x[rank : 2 * rank] + x[2 * rank :])

    for i in range(chunks):
        for c in loads[i]:
            c.wait()
        span = slice(i * chunk, (i + 1) * chunk)
        part = lax.dot_general(s3, dv[span, :], nt, preferred_element_type=f32)
        part += lax.dot_general(s3, ev[span, :], nt, preferred_element_type=f32)
        lpart[:, :, span] = fold(part).reshape(shares, per, chunk)

    pl.semaphore_wait(barrier, nr + nm - 2)

    def remote(src, dst, send, recv, to):
        return pltpu.make_async_remote_copy(
            src_ref=src, dst_ref=dst, send_sem=send, recv_sem=recv, device_id=to, device_id_type=MESH
        )

    def scatter(src, dst, send, recv):
        for d in range(1, nr):
            p = rep_at(d)

            @when(p < shares, everyone)
            def _():
                remote(src.at[p], dst.at[d], send.at[d], recv.at[d], (p, mdl)).start()

    def scatter_wait(src, dst, send, recv):
        for d in range(1, nr):

            @when(rep < shares, everyone)
            def _():
                remote(src.at[0], dst.at[d], send.at[d], recv.at[d], (rep, mdl)).wait_recv()

    def scatter_sent(src, dst, send, recv):
        for d in range(1, nr):
            p = rep_at(d)

            @when(p < shares, everyone)
            def _():
                remote(src.at[p], dst.at[d], send.at[d], recv.at[d], (p, mdl)).wait_send()

    def total(src, dst):
        t = src[rep]
        for d in range(1, nr):
            t = t + dst[d]
        return t / nr

    scatter(lpart, lrecv, ls_s, ls_r)
    scatter_wait(lpart, lrecv, ls_s, ls_r)

    @when(rep < shares, everyone)
    def _():
        lfull[rep] = total(lpart, lrecv)
        for d in range(1, nr):
            remote(lfull.at[rep], lfull.at[rep], lg_s.at[d], lg_r.at[d], (rep_at(d), mdl)).start()

    for d in range(1, nr):
        p = rep_at(-d)

        @when(p < shares, everyone)
        def _():
            remote(lfull.at[p], lfull.at[p], lg_s.at[d], lg_r.at[d], (rep, mdl)).wait_recv()

    left = lfull[...].reshape(rank, rows)

    gbuf[mdl] = lax.dot_general(left, left, nt, precision=highest, preferred_element_type=f32)
    for d in range(1, nm):
        remote(gbuf.at[mdl], gbuf.at[mdl], g_s.at[d], g_r.at[d], (rep, mdl_at(d))).start()

    l3 = jnp.concatenate(split3(left), axis=0)

    def product(cols):
        part = jnp.dot(l3, dv[:, cols], preferred_element_type=f32)
        part += jnp.dot(l3, ev[:, cols], preferred_element_type=f32)
        return fold(part).reshape(shares, per, cw)

    aligned = cw % 128 == 0
    if not aligned:
        for m in range(nm):
            rpart[m] = product(slice(m * cw, (m + 1) * cw))
    order = [lax.rem(rep + 1 + i, shares) for i in range(shares)]

    def to_mdl(d, i):
        j = order[i]
        return remote(
            rpart.at[mdl_at(d), j], rrecv.at[d, j], rs_s.at[d, i], rs_r.at[d, i], (rep, mdl_at(d))
        )

    for d in list(range(1, nm)) + [0]:
        if aligned:
            m = mdl_at(d)
            rpart[m] = product(pl.ds(pl.multiple_of(m * cw, 128), cw))
        if d > 0:
            for i in range(shares):
                to_mdl(d, i).start()

    for d in range(1, nm):
        p = mdl_at(-d)
        remote(gbuf.at[p], gbuf.at[p], g_s.at[d], g_r.at[d], (rep, mdl)).wait_recv()
    gram = gbuf[0]
    for m in range(1, nm):
        gram = gram + gbuf[m]
    y = lax.dot_general(
        left, inverse(gram, rank), (((0,), (0,)), ((), ())), precision=highest, preferred_element_type=f32
    )
    yh = y.astype(bf16).astype(f32)
    yl = y - yh
    y_ref[...] = jnp.concatenate([yh, yh, yl, yl], axis=1).astype(bf16)

    for i in range(shares):
        j = order[i]
        for d in range(1, nm):
            to_mdl(d, i).wait_recv()
        t = rpart[mdl, j]
        for d in range(1, nm):
            t = t + rrecv[d, j]
        rsum[j] = t
        for dr in range(1, nr):
            p = rep_at(dr)

            def send():
                remote(rsum.at[p], zrecv.at[dr], zs_s.at[dr], zs_r.at[dr], (p, mdl)).start()

            if everyone:
                if dr == i + 1:
                    send()
            elif i == shares - 1:
                pl.when(p < shares)(send)
    scatter_wait(rsum, zrecv, zs_s, zs_r)

    def forward(p, slot):
        for d in range(1, nm):
            remote(
                rfull.at[mdl, p], rfull.at[mdl, p], rg_s.at[d, slot], rg_r.at[d, slot], (rep, mdl_at(d))
            ).start()

    @when(rep < shares, everyone)
    def _():
        rfull[mdl, rep] = total(rsum, zrecv)
        for d in range(1, nr):
            remote(
                rfull.at[mdl, rep], rfull.at[mdl, rep], zg_s.at[d], zg_r.at[d], (rep_at(d), mdl)
            ).start()
        forward(rep, 0)

    for d in range(1, nr):
        p = rep_at(-d)

        @when(p < shares, everyone)
        def _():
            remote(rfull.at[mdl, p], rfull.at[mdl, p], zg_s.at[d], zg_r.at[d], (rep, mdl)).wait_recv()
            forward(p, d)

    for slot in range(nr):
        p = rep_at(-slot)

        @when(p < shares, everyone)
        def _():
            for d in range(1, nm):
                m = mdl_at(-d)
                remote(
                    rfull.at[m, p], rfull.at[m, p], rg_s.at[d, slot], rg_r.at[d, slot], (rep, mdl)
                ).wait_recv()

    for m in range(nm):
        hi, lo = split2(rfull[m].reshape(rank, cw))
        r_ref[:, m * cw : (m + 1) * cw] = jnp.concatenate([hi, lo, hi, lo], axis=0)
    for j in range(nr):

        @pl.when(rep == j)
        def _():
            own_ref[...] = r_ref[:, j * width : (j + 1) * width]

    scatter_sent(lpart, lrecv, ls_s, ls_r)
    scatter_sent(rsum, zrecv, zs_s, zs_r)

    @when(rep < shares, everyone)
    def _():
        for d in range(1, nr):
            remote(lfull.at[rep], lfull.at[rep], lg_s.at[d], lg_r.at[d], (rep_at(d), mdl)).wait_send()
            remote(
                rfull.at[mdl, rep], rfull.at[mdl, rep], zg_s.at[d], zg_r.at[d], (rep_at(d), mdl)
            ).wait_send()

    for d in range(1, nm):
        remote(gbuf.at[mdl], gbuf.at[mdl], g_s.at[d], g_r.at[d], (rep, mdl_at(d))).wait_send()
        for i in range(shares):
            to_mdl(d, i).wait_send()
        for slot in range(nr):
            p = rep_at(-slot)

            @when(p < shares, everyone)
            def _():
                remote(
                    rfull.at[mdl, p], rfull.at[mdl, p], rg_s.at[d, slot], rg_r.at[d, slot], (rep, mdl_at(d))
                ).wait_send()


def outputs(d_ref, e_ref, y_ref, r_ref, own_ref, m_ref, ne_ref, nm_ref, os_ref):
    approx = jnp.dot(y_ref[...], r_ref[...], preferred_element_type=f32)
    ne_ref[...] = ((d_ref[...].astype(f32) + e_ref[...].astype(f32)) - approx).astype(bf16)
    owned = jnp.dot(y_ref[...], own_ref[...], preferred_element_type=f32)
    new = 0.9 * m_ref[...] + owned
    nm_ref[...] = new
    os_ref[...] = 0.7 * (owned + 0.9 * new)


def body(nr, nm, deltas, errors, starts, momentum):
    deltas, errors = deltas[0], errors[0]
    rows, channels = deltas.shape
    rank = starts.shape[1]
    width = momentum.shape[1]
    shares = min(nr, max(rank // 8, 1))
    per = rank // shares
    cw = channels // nm
    chunk = 128 if rows % 128 == 0 else rows
    vmem = pl.BlockSpec(memory_space=pltpu.VMEM)
    hbm = pl.BlockSpec(memory_space=pl.ANY)
    dma = pltpu.SemaphoreType.DMA
    y, r, own = pl.pallas_call(
        functools.partial(factors, nr, nm, shares, chunk, width),
        name="factors",
        out_shape=(
            jax.ShapeDtypeStruct((rows, 4 * rank), bf16),
            jax.ShapeDtypeStruct((4 * rank, channels), bf16),
            jax.ShapeDtypeStruct((4 * rank, width), bf16),
        ),
        in_specs=[hbm, hbm, vmem],
        out_specs=(vmem, vmem, vmem),
        scratch_shapes=[
            pltpu.VMEM((rows, channels), bf16),
            pltpu.VMEM((rows, channels), bf16),
            pltpu.VMEM((shares, per, rows), f32),
            pltpu.VMEM((nr, per, rows), f32),
            pltpu.VMEM((shares, per, rows), f32),
            pltpu.VMEM((nm, rank, rank), f32),
            pltpu.VMEM((nm, shares, per, cw), f32),
            pltpu.VMEM((nm, shares, per, cw), f32),
            pltpu.VMEM((shares, per, cw), f32),
            pltpu.VMEM((nr, per, cw), f32),
            pltpu.VMEM((nm, shares, per, cw), f32),
            dma((2, rows // chunk)),
            dma((nr,)), dma((nr,)), dma((nr,)), dma((nr,)),
            dma((nm,)), dma((nm,)),
            dma((nm, shares)), dma((nm, shares)),
            dma((nr,)), dma((nr,)), dma((nr,)), dma((nr,)),
            dma((nm, nr)), dma((nm, nr)),
        ],
        compiler_params=pltpu.CompilerParams(
            collective_id=0, has_side_effects=True, vmem_limit_bytes=56 << 20
        ),
    )(deltas, errors, starts)

    def row_block(n):
        return pl.BlockSpec((chunk, n), lambda i: (i, 0))

    def whole(a):
        return pl.BlockSpec(a.shape, lambda i: (0, 0))

    new_errors, new_momentum, outer_step = pl.pallas_call(
        outputs,
        name="outputs",
        grid=(rows // chunk,),
        out_shape=(
            jax.ShapeDtypeStruct((rows, channels), bf16),
            jax.ShapeDtypeStruct((rows, width), f32),
            jax.ShapeDtypeStruct((rows, width), f32),
        ),
        in_specs=[
            row_block(channels), row_block(channels), row_block(4 * rank), whole(r), whole(own), row_block(width),
        ],
        out_specs=(row_block(channels), row_block(width), row_block(width)),
        compiler_params=pltpu.CompilerParams(vmem_limit_bytes=40 << 20),
    )(deltas, errors, y, r, own, momentum)
    return (new_errors[None], new_momentum, outer_step)


def solution(mesh):
    placed = (P("rep", "mdl", None), P("rep", "mdl", None), P(), P("mdl", "rep"))
    return jax.shard_map(
        functools.partial(body, mesh.shape["rep"], mesh.shape["mdl"]),
        mesh=mesh,
        in_specs=placed,
        out_specs=(P("rep", "mdl", None), P("mdl", "rep"), P("mdl", "rep")),
        check_vma=False,
    )
```

```python
import functools

import jax
import jax.numpy as jnp
from jax import lax
from jax.experimental import pallas as pl
from jax.experimental.pallas import tpu as pltpu
from jax.sharding import PartitionSpec as P

MESH = pl.DeviceIdType.MESH
highest = lax.Precision.HIGHEST
f32, bf16 = jnp.float32, jnp.bfloat16


def split3(x):
    hi = x.astype(bf16)
    rest = x - hi.astype(f32)
    mid = rest.astype(bf16)
    return hi, mid, (rest - mid.astype(f32)).astype(bf16)


def split2(x):
    hi = x.astype(bf16)
    return hi, (x - hi.astype(f32)).astype(bf16)


def when(cond, always):
    if always:
        return lambda f: f()
    return pl.when(cond)


def sweep(g, rank, first, last):
    rows = lax.broadcasted_iota(jnp.int32, (rank, rank), 0)
    cols = lax.broadcasted_iota(jnp.int32, (rank, rank), 1)
    for k in range(first, last):
        row = g[k : k + 1, :]
        col = g[:, k : k + 1]
        scale = 1.0 / g[k : k + 1, k : k + 1]
        rowk, colk = rows == k, cols == k
        left = jnp.where(rowk[:, :1], 0.0, col)
        kept = jnp.where(colk, 0.0, g)
        fill = jnp.where(colk[:1, :], scale, row * scale)
        g = jnp.where(rowk, fill, kept - left * fill)
    return g


def factors(
    nr, nm, shares, chunk, width,
    d_hbm, e_hbm, s_ref,
    fac_ref, dv, ev,
    lpart, lpair, lsum, lrecv, lfull, gbuf, rpart, rpair, rsum, rrecv, zsum, zrecv, rfull,
    in_sem, lp_s, lp_r, ls_s, ls_r, lg_s, lg_r, lf_s, lf_r, g_s, g_r,
    rp_s, rp_r, rs_s, rs_r, zs_s, zs_r, zg_s, zg_r, rg_s, rg_r, rf_s, rf_r,
):
    rep, mdl = lax.axis_index("rep"), lax.axis_index("mdl")
    z, core = lax.div(rep, 2), lax.rem(rep, 2)
    other = 1 - core
    nz = nr // 2
    rank = s_ref.shape[0]
    per = rank // (2 * shares)
    rows, channels = dv.shape
    cw = channels // nm
    chunks = rows // chunk
    everyone = shares == nz
    owner = when(z < shares, everyone)
    partner = (2 * z + other, mdl)

    def z_at(d):
        return lax.rem(z + d + nz, nz)

    def mdl_at(d):
        return lax.rem(mdl + d + nm, nm)

    def z_peer(d):
        return (2 * z_at(d) + core, mdl)

    def mdl_peer(d):
        return (rep, mdl_at(d))

    def remote(src, dst, send, recv, to):
        return pltpu.make_async_remote_copy(
            src_ref=src, dst_ref=dst, send_sem=send, recv_sem=recv, device_id=to, device_id_type=MESH
        )

    sent = []

    def start(copy, guard=None):
        if guard is None:
            copy().start()
            sent.append(lambda: copy().wait_send())
        else:
            guard(lambda: copy().start())
            sent.append(lambda: guard(lambda: copy().wait_send()))

    loads = []
    for i in range(chunks):
        span = pl.ds(i * chunk, chunk)
        pair = (
            pltpu.make_async_copy(d_hbm.at[span], dv.at[span], in_sem.at[0, i]),
            pltpu.make_async_copy(e_hbm.at[span], ev.at[span], in_sem.at[1, i]),
        )
        for c in pair:
            c.start()
        loads.append(pair)

    barrier = pltpu.get_barrier_semaphore()
    friends = [partner] + [z_peer(d) for d in range(1, nz)] + [mdl_peer(d) for d in range(1, nm)]
    for f in friends:
        pl.semaphore_signal(barrier, inc=1, device_id=f, device_id_type=MESH)

    s3 = jnp.concatenate(split3(s_ref[...]), axis=0)
    nt = (((1,), (1,)), ((), ()))

    def fold(x):
        return x[:rank] + (x[rank : 2 * rank] + x[2 * rank :])

    def lp(i):
        span = pl.ds(i * chunk, chunk)
        return remote(
            lpart.at[other, :, :, span], lpair.at[:, :, span], lp_s.at[i], lp_r.at[i], partner
        )

    def ls(d, i):
        span = pl.ds(i * chunk, chunk)
        return remote(
            lsum.at[z_at(d), :, span], lrecv.at[d, :, span], ls_s.at[d, i], ls_r.at[d, i], z_peer(d)
        )

    def left_pass(i):
        lp(i).wait_recv()
        span = slice(i * chunk, (i + 1) * chunk)
        lsum[:, :, span] = lpart[core, :, :, span] + lpair[:, :, span]
        for d in range(1, nz):
            start(functools.partial(ls, d, i), None if everyone else pl.when(z_at(d) < shares))

    for i in range(chunks):
        for c in loads[i]:
            c.wait()
        span = slice(i * chunk, (i + 1) * chunk)
        part = lax.dot_general(s3, dv[span, :], nt, preferred_element_type=f32)
        part += lax.dot_general(s3, ev[span, :], nt, preferred_element_type=f32)
        lpart[:, :, :, span] = fold(part).reshape(2, shares, per, chunk)
        if i == 0:
            pl.semaphore_wait(barrier, len(friends))
        start(functools.partial(lp, i))
        if i > 0:
            left_pass(i - 1)
    left_pass(chunks - 1)

    def lg(d):
        return remote(lfull.at[core, z], lfull.at[core, z], lg_s.at[d], lg_r.at[d], z_peer(d))

    def lf(d):
        p = z_at(-d)
        return remote(lfull.at[core, p], lfull.at[core, p], lf_s.at[d], lf_r.at[d], partner)

    def lf_in(d):
        p = z_at(-d)
        return remote(lfull.at[other, p], lfull.at[other, p], lf_s.at[d], lf_r.at[d], partner)

    @owner
    def _():
        for i in range(chunks):
            for d in range(1, nz):
                ls(d, i).wait_recv()
        t = lsum[z]
        for d in range(1, nz):
            t = t + lrecv[d]
        lfull[core, z] = t / nr

    for d in range(1, nz):
        start(functools.partial(lg, d), None if everyone else pl.when(z < shares))
    start(functools.partial(lf, 0), None if everyone else pl.when(z < shares))
    for d in range(1, nz):
        guard = None if everyone else pl.when(z_at(-d) < shares)

        def lg_in(d=d):
            p = z_at(-d)
            remote(lfull.at[core, p], lfull.at[core, p], lg_s.at[d], lg_r.at[d], partner).wait_recv()

        lg_in() if guard is None else guard(lg_in)
        start(functools.partial(lf, d), guard)
    for d in range(nz):
        when(z_at(-d) < shares, everyone)(lambda: lf_in(d).wait_recv())

    left = lfull[...].reshape(rank, rows)

    def gr(d):
        return remote(gbuf.at[mdl], gbuf.at[mdl], g_s.at[d], g_r.at[d], mdl_peer(d))

    gbuf[mdl] = lax.dot_general(left, left, nt, precision=highest, preferred_element_type=f32)
    for d in range(1, nm):
        start(functools.partial(gr, d))

    l3 = jnp.concatenate(split3(left), axis=0)

    def product(cols):
        part = jnp.dot(l3, dv[:, cols], preferred_element_type=f32)
        part += jnp.dot(l3, ev[:, cols], preferred_element_type=f32)
        return fold(part).reshape(2, shares, per, cw)

    aligned = cw % 128 == 0
    if not aligned:
        for m in range(nm):
            rpart[m] = product(slice(m * cw, (m + 1) * cw))
    order = [lax.rem(z + 1 + i, shares) for i in range(shares)]

    def rp(d):
        m = mdl_at(d)
        return remote(rpart.at[m, other], rpair.at[d], rp_s.at[d], rp_r.at[d], partner)

    def rs(d, i):
        j = order[i]
        return remote(rsum.at[d, j], rrecv.at[d, j], rs_s.at[d, i], rs_r.at[d, i], mdl_peer(d))

    def pair_pass(d):
        rp(d).wait_recv()
        rsum[d] = rpart[mdl_at(d), core] + rpair[d]
        if d > 0:
            for i in range(shares):
                start(functools.partial(rs, d, i))

    turns = list(range(1, nm)) + [0]
    for n, d in enumerate(turns):
        if aligned:
            m = mdl_at(d)
            rpart[m] = product(pl.ds(pl.multiple_of(m * cw, 128), cw))
        start(functools.partial(rp, d))
        if n > 0:
            pair_pass(turns[n - 1])
    pair_pass(turns[-1])

    for d in range(1, nm):
        p = mdl_at(-d)
        remote(gbuf.at[p], gbuf.at[p], g_s.at[d], g_r.at[d], partner).wait_recv()
    gram = gbuf[0]
    for m in range(1, nm):
        gram = gram + gbuf[m]
    cuts = [0, (rank * 20) // 64, (rank * 42) // 64, rank]
    gram = sweep(gram, rank, cuts[0], cuts[1])

    def zs(d):
        return remote(zsum.at[z_at(d)], zrecv.at[d], zs_s.at[d], zs_r.at[d], z_peer(d))

    for i in range(shares):
        j = order[i]
        for d in range(1, nm):
            rs(d, i).wait_recv()
        t = rsum[0, j]
        for d in range(1, nm):
            t = t + rrecv[d, j]
        zsum[j] = t
        if everyone and i + 1 < nz:
            start(functools.partial(zs, i + 1))
    if not everyone:
        for d in range(1, nz):
            start(functools.partial(zs, d), pl.when(z_at(d) < shares))

    gram = sweep(gram, rank, cuts[1], cuts[2])

    def zg(d):
        return remote(rfull.at[mdl, core, z], rfull.at[mdl, core, z], zg_s.at[d], zg_r.at[d], z_peer(d))

    def rg(d, slot):
        p = z_at(-slot)
        return remote(
            rfull.at[mdl, core, p], rfull.at[mdl, core, p], rg_s.at[d, slot], rg_r.at[d, slot], mdl_peer(d)
        )

    def rf(d, slot):
        m, p = mdl_at(-d), z_at(-slot)
        return remote(
            rfull.at[m, core, p], rfull.at[m, core, p], rf_s.at[d, slot], rf_r.at[d, slot], partner
        )

    def rf_in(d, slot):
        m, p = mdl_at(-d), z_at(-slot)
        return remote(
            rfull.at[m, other, p], rfull.at[m, other, p], rf_s.at[d, slot], rf_r.at[d, slot], partner
        )

    @owner
    def _():
        for d in range(1, nz):
            zs(d).wait_recv()
        t = zsum[z]
        for d in range(1, nz):
            t = t + zrecv[d]
        rfull[mdl, core, z] = t / nr

    def spread(slot, guard):
        for d in range(1, nm):
            start(functools.partial(rg, d, slot), guard)
        start(functools.partial(rf, 0, slot), guard)

    mine = None if everyone else pl.when(z < shares)
    for d in range(1, nz):
        start(functools.partial(zg, d), mine)
    spread(0, mine)

    gram = sweep(gram, rank, cuts[2], cuts[3])

    for slot in range(1, nz):
        guard = None if everyone else pl.when(z_at(-slot) < shares)

        def zg_in(slot=slot):
            p = z_at(-slot)
            remote(
                rfull.at[mdl, core, p], rfull.at[mdl, core, p], zg_s.at[slot], zg_r.at[slot], partner
            ).wait_recv()

        zg_in() if guard is None else guard(zg_in)
        spread(slot, guard)

    fac_ref[:, channels : channels + rows] = jnp.dot(gram, left, precision=highest, preferred_element_type=f32)

    for slot in range(nz):
        guard = None if everyone else pl.when(z_at(-slot) < shares)
        for d in range(1, nm):

            def rg_in(d=d, slot=slot):
                m, p = mdl_at(-d), z_at(-slot)
                remote(
                    rfull.at[m, core, p], rfull.at[m, core, p], rg_s.at[d, slot], rg_r.at[d, slot], partner
                ).wait_recv()

            rg_in() if guard is None else guard(rg_in)
            start(functools.partial(rf, d, slot), guard)
    for slot in range(nz):
        for d in range(nm):
            when(z_at(-slot) < shares, everyone)(lambda: rf_in(d, slot).wait_recv())

    for m in range(nm):
        fac_ref[:, m * cw : (m + 1) * cw] = rfull[m].reshape(rank, cw)
    for j in range(nr):

        @pl.when(rep == j)
        def _():
            fac_ref[:, channels + rows :] = fac_ref[:, j * width : (j + 1) * width]

    for f in sent:
        f()


def outputs(chunks, d_ref, e_ref, f_ref, m_ref, ne_ref, nm_ref, os_ref, right, own):
    step = pl.program_id(0)
    chunk, channels = d_ref.shape
    rows = chunk * chunks

    @pl.when(step == 0)
    def _():
        hi, lo = split2(f_ref[:, :channels])
        right[...] = jnp.concatenate([hi, lo, hi, lo], axis=0)
        hi, lo = split2(f_ref[:, channels + rows :])
        own[...] = jnp.concatenate([hi, lo, hi, lo], axis=0)

    start = channels if chunks == 1 else pl.multiple_of(channels + step * chunk, 128)
    hi, lo = split2(f_ref[:, pl.ds(start, chunk)])
    y = jnp.concatenate([hi, hi, lo, lo], axis=0)
    tn = (((0,), (0,)), ((), ()))
    approx = lax.dot_general(y, right[...], tn, preferred_element_type=f32)
    ne_ref[...] = ((d_ref[...].astype(f32) + e_ref[...].astype(f32)) - approx).astype(bf16)
    owned = lax.dot_general(own[...], y, tn, preferred_element_type=f32)
    new = 0.9 * m_ref[...] + owned
    nm_ref[...] = new
    os_ref[...] = 0.7 * (owned + 0.9 * new)


def body(nr, nm, deltas, errors, starts, momentum):
    deltas, errors, starts, momentum = deltas[0], errors[0], starts.T, momentum.T
    rows, channels = deltas.shape
    rank = starts.shape[0]
    width = momentum.shape[0]
    nz = nr // 2
    shares = min(nz, max(rank // 16, 1))
    per = rank // (2 * shares)
    cw = channels // nm
    chunk = 128 if rows % 128 == 0 else rows
    chunks = rows // chunk
    vmem = pl.BlockSpec(memory_space=pltpu.VMEM)
    hbm = pl.BlockSpec(memory_space=pltpu.HBM)
    dma = pltpu.SemaphoreType.DMA
    fac, deltas, errors = pl.pallas_call(
        functools.partial(factors, nr, nm, shares, chunk, width),
        name="factors",
        out_shape=(
            jax.ShapeDtypeStruct((rank, channels + rows + width), f32),
            jax.ShapeDtypeStruct((rows, channels), bf16),
            jax.ShapeDtypeStruct((rows, channels), bf16),
        ),
        in_specs=[hbm, hbm, vmem],
        out_specs=(vmem, vmem, vmem),
        scratch_shapes=[
            pltpu.VMEM((2, shares, per, rows), f32),
            pltpu.VMEM((shares, per, rows), f32),
            pltpu.VMEM((shares, per, rows), f32),
            pltpu.VMEM((nz, per, rows), f32),
            pltpu.VMEM((2, shares, per, rows), f32),
            pltpu.VMEM((nm, rank, rank), f32),
            pltpu.VMEM((nm, 2, shares, per, cw), f32),
            pltpu.VMEM((nm, shares, per, cw), f32),
            pltpu.VMEM((nm, shares, per, cw), f32),
            pltpu.VMEM((nm, shares, per, cw), f32),
            pltpu.VMEM((shares, per, cw), f32),
            pltpu.VMEM((nz, per, cw), f32),
            pltpu.VMEM((nm, 2, shares, per, cw), f32),
            dma((2, chunks)),
            dma((chunks,)), dma((chunks,)), dma((nz, chunks)), dma((nz, chunks)),
            dma((nz,)), dma((nz,)), dma((nz,)), dma((nz,)),
            dma((nm,)), dma((nm,)),
            dma((nm,)), dma((nm,)), dma((nm, shares)), dma((nm, shares)),
            dma((nz,)), dma((nz,)), dma((nz,)), dma((nz,)),
            dma((nm, nz)), dma((nm, nz)), dma((nm, nz)), dma((nm, nz)),
        ],
        compiler_params=pltpu.CompilerParams(
            collective_id=0, has_side_effects=True, vmem_limit_bytes=46 << 20
        ),
    )(deltas, errors, starts)

    def row_block(n):
        return pl.BlockSpec((chunk, n), lambda i: (i, 0))

    def column_block(n):
        return pl.BlockSpec((n, chunk), lambda i: (0, i))

    new_errors, new_momentum, outer_step = pl.pallas_call(
        functools.partial(outputs, chunks),
        name="outputs",
        grid=(rows // chunk,),
        out_shape=(
            jax.ShapeDtypeStruct((rows, channels), bf16),
            jax.ShapeDtypeStruct((width, rows), f32),
            jax.ShapeDtypeStruct((width, rows), f32),
        ),
        in_specs=[
            row_block(channels), row_block(channels), pl.BlockSpec(fac.shape, lambda i: (0, 0)), column_block(width),
        ],
        out_specs=(row_block(channels), column_block(width), column_block(width)),
        scratch_shapes=[pltpu.VMEM((4 * rank, channels), bf16), pltpu.VMEM((4 * rank, width), bf16)],
        compiler_params=pltpu.CompilerParams(vmem_limit_bytes=40 << 20),
    )(deltas, errors, fac, momentum)
    return (new_errors[None], new_momentum.T, outer_step.T)


def solution(mesh):
    placed = (P("rep", "mdl", None), P("rep", "mdl", None), P(), P("mdl", "rep"))
    return jax.shard_map(
        functools.partial(body, mesh.shape["rep"], mesh.shape["mdl"]),
        mesh=mesh,
        in_specs=placed,
        out_specs=(P("rep", "mdl", None), P("mdl", "rep"), P("mdl", "rep")),
        check_vma=False,
    )
```
